32 devices in a mesh: grp: 2 (over x), ep: 16 (over z, y, core).
Axes of the slice: x: 2, y: 2, z: 4, core: 2. Of those that a mesh axis runs over, the one named last changes fastest.
Arguments:
- hidden_in: bfloat16 [2, 1024, 2048], P(None, ('grp', 'ep')), parts along dimension 1, may hold values from -12 to 12
- expert_ids: int32 [2, 1024, 8], P(None, ('grp', 'ep')), parts along dimension 1, may hold values from 0 to 15, all different within a row; in each aligned block of 32 rows (0 to 31, 32 to 63, ..., all dimensions but the last counted through in order) at most 32 rows name the same one
- route_share: int32 [2, 1024, 8], P(None, ('grp', 'ep')), parts along dimension 1, may hold values from 4 to 28
- norm_gain: float32 [2048], replicated, may hold values from 0.1 to 1.9
- gate_weight: bfloat16 [16, 2048, 768], P('ep'), may hold values from -0.125 to 0.125
- up_weight: bfloat16 [16, 2048, 768], P('ep'), may hold values from -0.125 to 0.125
- down_weight: bfloat16 [16, 768, 2048], P('ep'), may hold values from -0.21875 to 0.21875
- exponent_table: int32 [16, 3, 6], P('ep'), may hold values from -2 to 1
Outputs:
- mixed_out: bfloat16 [2, 1024, 2048], P(None, ('grp', 'ep')), parts along dimension 1
The draws below stay inside these ranges and needn't reach their ends.
There are 2 independent parts, one for each index of `grp`. The reference program is written for one: setup_inputs(seed, part) draws one part's arguments, and reference() takes and returns one part's arrays. A program takes and returns all parts, laid end to end along the dimension named above; an argument that names none is the same for every part. Nothing has to cross between parts.
Inputs may be any that keep to these rules, and one draw needn't show every extreme that they name: `expert_ids`: each row names 8 different experts. Within each micro-batch, in each aligned block of 32 rows, no expert is named by more than 32 rows, and in some blocks one expert is named by exactly 32 rows.
All inputs are finite; a program needn't handle non-finite values.
Results may differ from the reference program's by a relative error of at most 0.0044.
Values may be sent and summed in bfloat16 or wider, within the bound.
A program may use at most 64 MiB of HBM per device.

```python
import math
import jax
import jax.numpy as jnp
import numpy as np
from jax import lax

D = 2048
FF = 768
TOP = 8
SCALE_GROUP = 128
MICRO = 2
ROWS_DEV = 32
EXPERTS = 16
ROWS = 512
CAP = 32
N_EP = 16


def draw_hidden_in(key, part):
    key_base, key_rows, key_cols = jax.random.split(jax.random.fold_in(key, 17), 3)
    row_scale = jnp.exp(jax.random.uniform(key_rows, (MICRO, ROWS, 1), jnp.float32, math.log(0.3), math.log(3.0)))
    col_scale = jnp.exp(jax.random.uniform(key_cols, (1, 1, D), jnp.float32, math.log(0.5), math.log(2.0)))
    base = jax.random.normal(key_base, (MICRO, ROWS, D), jnp.float32)
    values = jnp.clip(base * row_scale * col_scale, -12.0, 12.0)
    return values.astype(jnp.bfloat16)


def touch_ends(result, own_key, low, largest):
    place = [jax.random.randint(jax.random.fold_in(own_key, axis), (), 0, length) for axis, length in enumerate(result.shape)]
    main_axis = result.shape.index(max(result.shape))
    beside = place[:main_axis] + [(place[main_axis] + 1) % result.shape[main_axis]] + place[main_axis + 1:]
    return result.at[tuple(place)].set(low).at[tuple(beside)].set(largest)


def steps_of(stream_key, dims, cuts, low, largest):
    def one(axis_at, parts):
        draws = jax.random.uniform(jax.random.fold_in(jax.random.fold_in(stream_key, 6), axis_at), (parts,), jnp.float32, low / len(cuts), largest / len(cuts))
        return jnp.repeat(jnp.exp(draws), dims[axis_at] // parts).reshape((-1,) + (1,) * (len(dims) - axis_at - 1))

    loudness = one(*cuts[0])
    for cut in cuts[1:]:
        loudness = loudness * one(*cut)
    return loudness


def assign_block(key, own, number, rows, count, top, most, lean):
    order = jax.random.permutation(key, count)
    crowded, common = load_shares(count, rows * top, most, lean, True), load_shares(count, rows * top, most, lean, False)
    places = jnp.arange(count)

    def named(tallies, offset_by):
        used = int((tallies > 0).sum())
        fixed = max(1, used // 4)
        passed = fixed + (places - fixed + offset_by * (used - fixed)) % max(1, count - fixed)
        return jnp.zeros((count,), jnp.int32).at[order[jnp.where(places < fixed, places, passed)]].set(jnp.asarray(tallies, jnp.int32))

    tallies = jnp.where(number % 4 == 0, named(crowded, number // 4), named(common, number - number // 4 - 1))
    mixed = jax.random.permutation(jax.random.fold_in(own, 3), count)
    source_of, sink = mixed[0:count // 2 * 2:2], mixed[1:count // 2 * 2:2]
    room = jnp.minimum(tallies[source_of] - 1, most - tallies[sink]) // 2
    room = jnp.where((source_of == order[0]) | (sink == order[0]) | (tallies[sink] == 0), 0, jnp.maximum(room, 0))
    passed = jax.random.randint(jax.random.fold_in(own, 4), (count // 2,), 0, 1 << 20) % (room + 1)
    tallies = tallies.at[source_of].add(-passed).at[sink].add(passed)
    members = jnp.searchsorted(jnp.cumsum(tallies), jnp.arange(rows * top), side="right").astype(jnp.int32)
    table = members.reshape(top, rows).T
    table = table[jax.random.permutation(jax.random.fold_in(own, 1), rows)]
    offset_by = jax.random.randint(jax.random.fold_in(own, 2), (rows, 1), 0, top)
    return jnp.take_along_axis(table, (jnp.arange(top)[None, :] + offset_by) % top, axis=1)


def load_shares(count, total, reach, lean, full):
    weights = [(1 << 20) // math.isqrt(rank ** lean) + 1 for rank in range(1, count + 1)]
    largest = reach if full else min(reach, max(-(-total // count), total * weights[0] // sum(weights)))
    least = 1 if total - largest >= count - 1 else 0
    given, surplus = [largest] + [least] * (count - 1), total - largest - least * (count - 1)
    while surplus > 0:
        free = [i for i in range(1, count) if given[i] < largest] or [i for i in range(1, count) if given[i] < reach]
        pool, remaining = sum([weights[i] for i in free]), surplus
        for i in free:
            extra = min(reach - given[i], max(1, remaining * weights[i] // pool), surplus)
            given[i] = given[i] + extra
            surplus = surplus - extra
    return np.array(given)


def gaussian(stream_key, extent, scale, most, shards=(), kind=jnp.bfloat16):
    values = jax.random.normal(stream_key, extent, jnp.float32) * scale
    if len(shards) > 0:
        values = steps_of(stream_key, extent, shards, -0.22, 0.18) * values
    return jnp.clip(values, min=-most, max=most).astype(kind)


def setup_inputs(seed: int = 0, part: int = 0) -> dict:
    splits = jax.random.split(jax.random.key(seed), 9)
    part_keys = jax.random.split(jax.random.fold_in(splits[8], part), 9)
    hidden_in = draw_hidden_in(jax.random.fold_in(jax.random.fold_in(splits[8], part), 71), part)
    expert_ids_keys = jax.random.split(jax.random.fold_in(part_keys[1], 1), MICRO * ROWS // ROWS_DEV)
    expert_ids_turns = jax.random.permutation(jax.random.fold_in(part_keys[1], 3), MICRO * ROWS // ROWS_DEV)
    expert_ids = jax.vmap(lambda own, number: assign_block(jax.random.fold_in(part_keys[1], 2), own, number, ROWS_DEV, EXPERTS, TOP, CAP, 2))(expert_ids_keys, expert_ids_turns).reshape((MICRO, ROWS, TOP))
    route_share = touch_ends(jax.random.randint(part_keys[2], (MICRO, ROWS, TOP), 4, 29), jax.random.fold_in(part_keys[2], 1), 4, 28).astype(jnp.int32)
    norm_gain = jnp.clip(1.0 + 0.18 * jax.random.normal(splits[3], (D,), jnp.float32), 0.1, 1.9)
    gate_weight = gaussian(splits[4], (EXPERTS, D, FF), D ** -0.5, 0.125, ((0, 16),))
    up_weight = gaussian(splits[5], (EXPERTS, D, FF), D ** -0.5, 0.125, ((0, 16),))
    down_weight = gaussian(splits[6], (EXPERTS, FF, D), FF ** -0.5, 0.21875, ((0, 16),))
    exponent_table = touch_ends(jax.random.randint(splits[7], (EXPERTS, 3, FF // SCALE_GROUP), -2, 2), jax.random.fold_in(splits[7], 1), -2, 1).astype(jnp.int32)
    return {"hidden_in": hidden_in, "expert_ids": expert_ids, "route_share": route_share, "norm_gain": norm_gain, "gate_weight": gate_weight, "up_weight": up_weight, "down_weight": down_weight, "exponent_table": exponent_table}


def normalize(hidden_in, norm_gain):
    values = hidden_in.astype(jnp.float32)
    power = lax.optimization_barrier(jnp.mean(values * values, axis=-1, keepdims=True))
    return (values * lax.rsqrt(power + 1e-06) * norm_gain.astype(jnp.float32)).astype(jnp.bfloat16)

def expert_ffn(operands):
    block_of_rows, gate_matrix, up_matrix, down_mat, scale_exponents = operands
    scale_factors = jnp.repeat(jnp.exp2(scale_exponents.astype(jnp.float32)), SCALE_GROUP, axis=1)
    gate_output = jnp.dot(block_of_rows, gate_matrix, preferred_element_type=jnp.float32) * scale_factors[0]
    up_output = jnp.dot(block_of_rows, up_matrix, preferred_element_type=jnp.float32) * scale_factors[1]
    hidden_state = (jax.nn.silu(gate_output) * up_output * scale_factors[2]).astype(jnp.bfloat16)
    return jnp.dot(hidden_state, down_mat, preferred_element_type=jnp.float32).astype(jnp.bfloat16)

def slot_places(chosen):
    grouped = chosen.reshape(N_EP, ROWS_DEV * TOP)
    onehot = (grouped[:, :, None] == jnp.arange(EXPERTS, dtype=jnp.int32)[None, None, :]).astype(jnp.int32)
    running = jnp.cumsum(onehot, axis=1) - 1
    position = lax.optimization_barrier(jnp.sum(running * onehot, axis=2)).astype(jnp.int32)
    return position.reshape(ROWS, TOP)

def reference(hidden_in, expert_ids, route_share, norm_gain, gate_weight, up_weight, down_weight, exponent_table):
    outputs = []
    for batch in range(MICRO):
        rows_in = hidden_in[batch]
        chosen = expert_ids[batch].astype(jnp.int32)
        normed = normalize(rows_in, norm_gain)
        position = slot_places(chosen)
        source = (jnp.arange(ROWS, dtype=jnp.int32) // ROWS_DEV)[:, None]
        column = (source * CAP + position).astype(jnp.int32)
        spread_rows = jnp.broadcast_to(normed[:, None, :], (ROWS, TOP, D))
        buffer = jnp.zeros((EXPERTS, N_EP * CAP, D), jnp.bfloat16).at[chosen, column].set(spread_rows)
        results = lax.map(expert_ffn, (buffer, gate_weight, up_weight, down_weight, exponent_table))
        picked = results[chosen, column]
        shares = route_share[batch].astype(jnp.float32) / 64.0
        mixed = jnp.einsum('rk,rkd->rd', shares, picked.astype(jnp.float32))
        outputs.append((rows_in.astype(jnp.float32) + mixed).astype(jnp.bfloat16))
    return jnp.stack(outputs)
```

```python
import functools

import jax
import jax.numpy as jnp
from jax import lax
from jax.experimental import pallas as pl
from jax.experimental.pallas import tpu as pltpu
from jax.sharding import PartitionSpec as P

SCALE_GROUP = 128
LANES = 128
INNER = 4
VMEM_BYTES = 67_043_328
MESH = pl.DeviceIdType.MESH
EXP_DEV = 1


def normalize(rows_in, norm_gain):
    values = rows_in.astype(jnp.float32)
    power = jnp.mean(values * values, axis=-1, keepdims=True)
    return (values * lax.rsqrt(power + 1e-06) * norm_gain).astype(jnp.bfloat16)


def local(
    hidden_in,
    expert_ids,
    route_share,
    norm_gain,
    gate_weight,
    up_weight,
    down_weight,
    exponent_table,
):
    owners = lax.axis_size("ep")
    experts = owners * EXP_DEV
    batches, dev_rows, fanout = expert_ids.shape
    model_width = hidden_in.shape[2]
    capacity = min(dev_rows, 2 * dev_rows * fanout // experts)
    scale_factors = jnp.repeat(jnp.exp2(exponent_table[0].astype(jnp.float32)), SCALE_GROUP, axis=1)
    gate_matrix = gate_weight[0]
    up_matrix = up_weight[0]
    down_mat = down_weight[0]
    slot_ids = jnp.arange(experts * capacity, dtype=jnp.int32)
    expert_range = jnp.arange(experts, dtype=jnp.int32)

    def expert_rows(block_of_rows):
        gate_output = (
            jnp.dot(block_of_rows, gate_matrix, preferred_element_type=jnp.float32)
            * scale_factors[0]
        )
        up_output = (
            jnp.dot(block_of_rows, up_matrix, preferred_element_type=jnp.float32) * scale_factors[1]
        )
        hidden_state = (jax.nn.silu(gate_output) * up_output * scale_factors[2]).astype(
            jnp.bfloat16
        )
        return jnp.dot(hidden_state, down_mat, preferred_element_type=jnp.float32).astype(
            jnp.bfloat16
        )

    def mixing_for(batch):
        flat_ids = expert_ids[batch].reshape(-1)
        onehot = (flat_ids[:, None] == expert_range[None, :]).astype(jnp.int32)
        position = jnp.sum((jnp.cumsum(onehot, axis=0) - 1) * onehot, axis=1)
        slot_of = (flat_ids * capacity + position).reshape(dev_rows, fanout)
        matches = slot_of[:, :, None] == slot_ids[None, None, :]
        shares = route_share[batch].astype(jnp.float32) / 64.0
        mixing = jnp.sum(jnp.where(matches, shares[:, :, None], 0.0), axis=1).astype(jnp.bfloat16)
        picker = jnp.any(matches, axis=1).T.astype(jnp.bfloat16)
        return (mixing, picker)

    def serve(batch_list):
        count = len(batch_list)
        mixings = []
        pickers = []
        for batch in batch_list:
            mixing, picker = mixing_for(batch)
            mixings.append(mixing)
            pickers.append(picker)
        normed_list = [normalize(hidden_in[batch], norm_gain) for batch in batch_list]
        local_rows = normed_list[0]
        local_ids = jnp.concatenate([expert_ids[batch] for batch in batch_list], axis=0)
        all_rows = lax.all_gather(local_rows, "ep", axis=0, tiled=True)
        all_ids = lax.all_gather(local_ids, "ep", axis=0, tiled=True)
        all_rows = all_rows.reshape(owners, count, dev_rows, model_width)
        all_ids = all_ids.reshape(owners, count, dev_rows, fanout)
        owner = lax.axis_index("ep")
        block_base = (jnp.arange(owners, dtype=jnp.int32) * capacity)[:, None]
        ids_here = all_ids[:, 0].reshape(owners, dev_rows * fanout)
        mine = (ids_here == owner).astype(jnp.int32)
        place = jnp.where(mine > 0, block_base + jnp.cumsum(mine, axis=1) - 1, -1)
        place = place.reshape(owners * dev_rows, fanout)
        chooser = jnp.any(place[:, :, None] == slot_ids[None, None, :], axis=1).T.astype(
            jnp.bfloat16
        )
        rows_here = all_rows[:, 0].reshape(owners * dev_rows, model_width)
        built = jnp.dot(chooser, rows_here, preferred_element_type=jnp.float32).astype(jnp.bfloat16)
        buffers = built.reshape(experts, capacity, model_width)
        produced = expert_rows(buffers.reshape(-1, model_width)).reshape(
            experts, count * capacity, model_width
        )
        returned = lax.all_to_all(produced, "ep", split_axis=0, concat_axis=0, tiled=True)
        return (returned, mixings)

    outputs = []
    for batch in range(batches):
        returned, mixings = serve([batch])
        gathered = returned.reshape(experts * capacity, model_width)
        mixed = jnp.dot(mixings[0], gathered, preferred_element_type=jnp.float32)
        outputs.append((hidden_in[batch].astype(jnp.float32) + mixed).astype(jnp.bfloat16))
    return jnp.stack(outputs)


def visit_order(groups):
    return [sorted(range(groups), key=lambda other: (abs(other - own), other < own)) for own in range(groups)]


def expert_kernel(
    groups,
    x_ref,
    ids_ref,
    share_ref,
    gain_ref,
    gate_hbm,
    up_hbm,
    down_hbm,
    exps_ref,
    out_ref,
    rows,
    gate,
    up,
    down,
    scales,
    hidden,
    part,
    core_in,
    y_out,
    y_in,
    keep,
    z_out,
    z_in,
    weight_sem,
    rows_sent,
    rows_got,
    core_sent,
    core_got,
    y_sent,
    y_got,
    z_sent,
    z_got,
):
    batches, dev_rows, width = x_ref.shape
    fanout = ids_ref.shape[2]
    units = groups * batches
    chunk_rows = INNER * dev_rows
    ffw = gate.shape[1]
    me = lax.axis_index("ep")
    core = lax.rem(me, 2)
    row = lax.rem(lax.div(me, 2), 2)
    place = lax.div(me, INNER)
    here = row * 2 + core
    sib = me + 1 - 2 * core
    across = me + 2 - 4 * row
    above = me + INNER
    below = me - INNER
    has_above = place < groups - 1
    has_below = place > 0

    weight_copies = [
        pltpu.make_async_copy(gate_hbm.at[0], gate, weight_sem.at[0]),
        pltpu.make_async_copy(up_hbm.at[0], up, weight_sem.at[1]),
        pltpu.make_async_copy(down_hbm.at[0], down, weight_sem.at[2]),
    ]
    for copy in weight_copies:
        copy.start()

    barrier = pltpu.get_barrier_semaphore()

    def greet(device):
        pl.semaphore_signal(barrier, inc=1, device_id={"ep": device}, device_id_type=MESH)

    greet(sib)
    greet(across)
    pl.when(has_above)(lambda: greet(above))
    pl.when(has_below)(lambda: greet(below))

    def remote(src, dst, sent, got, device):
        return pltpu.make_async_remote_copy(
            src_ref=src,
            dst_ref=dst,
            send_sem=sent,
            recv_sem=got,
            device_id={"ep": device},
            device_id_type=MESH,
        )

    def rows_copy(outer, batch, inner, kind, device):
        ref = rows.at[outer, batch, inner]
        return remote(ref, ref, rows_sent.at[outer, batch, kind], rows_got.at[outer, batch, inner], device)

    lane = lax.broadcasted_iota(jnp.int32, (dev_rows, LANES), 1)
    for batch in range(batches):
        values = x_ref[batch].astype(jnp.float32)
        power = jnp.mean(values * values, axis=-1, keepdims=True)
        normed = (values * lax.rsqrt(power + 1e-06) * gain_ref[...]).astype(jnp.bfloat16)
        mixing = jnp.zeros((dev_rows, LANES), jnp.float32)
        for k in range(fanout):
            share = share_ref[batch, :, k : k + 1].astype(jnp.float32) / 64.0
            mixing += jnp.where(ids_ref[batch, :, k : k + 1] == lane, share, 0.0)
        rows[place, batch, here, :, :width] = normed
        rows[place, batch, here, :, width:] = mixing.astype(jnp.bfloat16)
        if batch == 0:
            pl.semaphore_wait(barrier, 2 + has_above.astype(jnp.int32) + has_below.astype(jnp.int32))
        pl.when(has_above)(lambda: rows_copy(place, batch, here, 0, above).start())
        pl.when(has_below)(lambda: rows_copy(place, batch, here, 1, below).start())
        rows_copy(place, batch, here, 3, across).start()
        rows_copy(place, batch, here, 2, sib).start()

    for m in range(3):
        for j in range(ffw // SCALE_GROUP):
            power_of = jnp.full((1, SCALE_GROUP), exps_ref[0, m, j], jnp.int32).astype(jnp.float32)
            scales[m : m + 1, j * SCALE_GROUP : (j + 1) * SCALE_GROUP] = jnp.exp2(power_of)

    table = visit_order(groups)

    def unit_of(u):
        step = lax.div(u, batches)
        batch = lax.rem(u, batches)
        outer = jnp.int32(0)
        for own in range(groups):
            for at in range(groups):
                outer = jnp.where((place == own) & (step == at), jnp.int32(table[own][at]), outer)
        return outer, batch

    other_row = (1 - row) * 2 + core

    def z_relay(u):
        outer, batch = unit_of(u)
        rows_copy(outer, batch, here, 0, sib).wait_recv()
        pl.when((outer < place) & has_above)(lambda: rows_copy(outer, batch, here, 0, above).start())
        pl.when((outer > place) & has_below)(lambda: rows_copy(outer, batch, here, 1, below).start())
        rows_copy(outer, batch, here, 3, across).start()
        rows_copy(outer, batch, here, 2, sib).start()

    def y_relay(u):
        outer, batch = unit_of(u)
        rows_copy(outer, batch, other_row, 4, sib).wait_recv()
        rows_copy(outer, batch, other_row, 4, sib).start()

    def arrived(u):
        outer, batch = unit_of(u)
        rows_copy(outer, batch, row * 2 + 1 - core, 2, sib).wait_recv()
        rows_copy(outer, batch, (1 - row) * 2 + 1 - core, 4, sib).wait_recv()

    def compute_hidden(u):
        outer, batch = unit_of(u)
        block = rows[outer, batch, :, :, :width].reshape(chunk_rows, width)
        tile = 256
        for at in range(0, ffw, tile):
            cols = slice(at, at + tile)
            gated = jnp.dot(block, gate[:, cols], preferred_element_type=jnp.float32) * scales[0:1, cols]
            upped = jnp.dot(block, up[:, cols], preferred_element_type=jnp.float32) * scales[1:2, cols]
            hidden[:, cols] = (jax.nn.silu(gated) * upped * scales[2:3, cols]).astype(jnp.bfloat16)

    def core_copy(outer, batch, which):
        return remote(
            part.at[outer, batch, which * 2 + 1 - core],
            core_in.at[outer, batch, which],
            core_sent.at[outer, batch, which],
            core_got.at[outer, batch, which],
            sib,
        )

    def compute_part(u):
        outer, batch = unit_of(u)
        mixing = rows[outer, batch, :, :, width:].reshape(chunk_rows, LANES).astype(jnp.float32)
        wide_lane = lax.broadcasted_iota(jnp.int32, (chunk_rows, LANES), 1)
        share = jnp.sum(jnp.where(wide_lane == me, mixing, 0.0), axis=1, keepdims=True)
        tile = 512 if width % 512 == 0 else width
        for at in range(0, width, tile):
            cols = slice(at, at + tile)
            produced = jnp.dot(hidden[...], down[:, cols], preferred_element_type=jnp.float32) * share
            part[outer, batch, :, :, cols] = produced.astype(jnp.bfloat16).reshape(INNER, dev_rows, tile)
        core_copy(outer, batch, 1 - row).start()
        core_copy(outer, batch, row).start()

    def y_copy(outer, batch):
        return remote(
            y_out.at[outer, batch],
            y_in.at[outer, batch],
            y_sent.at[outer, batch],
            y_got.at[outer, batch],
            across,
        )

    def core_reduce(u):
        outer, batch = unit_of(u)
        core_copy(outer, batch, 1 - row).wait_recv()
        summed = part[outer, batch, other_row].astype(jnp.float32) + core_in[outer, batch, 1 - row].astype(jnp.float32)
        y_out[outer, batch] = summed.astype(jnp.bfloat16)
        y_copy(outer, batch).start()
        core_copy(outer, batch, row).wait_recv()
        keep[outer, batch] = part[outer, batch, here].astype(jnp.float32) + core_in[outer, batch, row].astype(
            jnp.float32
        )

    def y_reduce(u):
        outer, batch = unit_of(u)
        y_copy(outer, batch).wait_recv()
        keep[outer, batch] += y_in[outer, batch].astype(jnp.float32)

    def z_copy(way, outer, batch, device):
        return remote(
            z_out.at[outer, batch],
            z_in.at[way, outer, batch],
            z_sent.at[outer, batch],
            z_got.at[way, outer, batch],
            device,
        )

    def chain(u):
        step = lax.div(u, batches)
        batch = lax.rem(u, batches)
        for way, outer, active, more, device in (
            (0, step, step > place, has_below, above),
            (1, groups - 1 - step, groups - 1 - step < place, has_above, below),
        ):

            @pl.when(active & more)
            def _():
                z_copy(way, outer, batch, sib).wait_recv()
                summed = keep[outer, batch] + z_in[way, outer, batch].astype(jnp.float32)
                z_out[outer, batch] = summed.astype(jnp.bfloat16)
                z_copy(way, outer, batch, device).start()

            @pl.when(active & jnp.logical_not(more))
            def _():
                z_out[outer, batch] = keep[outer, batch].astype(jnp.bfloat16)
                z_copy(way, outer, batch, device).start()

    y_relay(0)
    for copy in weight_copies:
        copy.wait()

    @pl.loop(0, units + 2)
    def _(u):
        @pl.when(u < units)
        def _():
            arrived(u)
            compute_hidden(u)

        pl.when(u + 1 < units)(lambda: y_relay(u + 1))
        pl.when(u + batches < units)(lambda: z_relay(u + batches))
        pl.when(u < units)(lambda: compute_part(u))
        pl.when((u >= 1) & (u <= units))(lambda: core_reduce(u - 1))

        @pl.when(u >= 2)
        def _():
            y_reduce(u - 2)
            chain(u - 2)

    for batch in range(batches):

        @pl.when(has_below)
        def _():
            z_copy(0, place, batch, sib).wait_recv()
            keep[place, batch] += z_in[0, place, batch].astype(jnp.float32)

        @pl.when(has_above)
        def _():
            z_copy(1, place, batch, sib).wait_recv()
            keep[place, batch] += z_in[1, place, batch].astype(jnp.float32)

        out_ref[batch] = (x_ref[batch].astype(jnp.float32) + keep[place, batch]).astype(jnp.bfloat16)

    @pl.loop(0, units)
    def _(u):
        outer = lax.div(u, batches)
        batch = lax.rem(u, batches)
        pl.when((outer <= place) & has_above)(lambda: rows_copy(outer, batch, here, 0, sib).wait_send())
        pl.when((outer >= place) & has_below)(lambda: rows_copy(outer, batch, here, 1, sib).wait_send())
        for kind in (2, 3, 4):
            rows_copy(outer, batch, here, kind, sib).wait_send()
        core_copy(outer, batch, 0).wait_send()
        core_copy(outer, batch, 1).wait_send()
        y_copy(outer, batch).wait_send()
        pl.when(outer != place)(lambda: z_copy(0, outer, batch, sib).wait_send())


def kernel_scratch(groups, batches, dev_rows, width, ffw):
    block = (groups, batches)
    bf16 = jnp.bfloat16
    buffers = [
        ((*block, INNER, dev_rows, width + LANES), bf16),
        ((width, ffw), bf16),
        ((width, ffw), bf16),
        ((ffw, width), bf16),
        ((8, ffw), jnp.float32),
        ((INNER * dev_rows, ffw), bf16),
        ((*block, INNER, dev_rows, width), bf16),
        ((*block, 2, dev_rows, width), bf16),
        ((*block, dev_rows, width), bf16),
        ((*block, dev_rows, width), bf16),
        ((*block, dev_rows, width), jnp.float32),
        ((*block, dev_rows, width), bf16),
        ((2, *block, dev_rows, width), bf16),
    ]
    semaphores = [(3,), (*block, 5), (*block, INNER), (*block, 2), (*block, 2), block, block, block, (2, *block)]
    return buffers, semaphores


def fused(groups, buffers, semaphores, hidden_in, expert_ids, route_share, norm_gain, gate_weight, up_weight, down_weight, exponent_table):
    vmem = pl.BlockSpec(memory_space=pltpu.VMEM)
    anywhere = pl.BlockSpec(memory_space=pl.ANY)
    return pl.pallas_call(
        functools.partial(expert_kernel, groups),
        out_shape=jax.ShapeDtypeStruct(hidden_in.shape, hidden_in.dtype),
        in_specs=[vmem, vmem, vmem, vmem, anywhere, anywhere, anywhere, pl.BlockSpec(memory_space=pltpu.SMEM)],
        out_specs=vmem,
        scratch_shapes=[pltpu.VMEM(shape, kind) for shape, kind in buffers]
        + [pltpu.SemaphoreType.DMA(shape) for shape in semaphores],
        compiler_params=pltpu.CompilerParams(
            collective_id=0, has_side_effects=True, vmem_limit_bytes=VMEM_BYTES * 15 // 16
        ),
    )(hidden_in, expert_ids, route_share, norm_gain[None, :], gate_weight, up_weight, down_weight, exponent_table)


def serve_local(*args):
    hidden_in, gate_weight = args[0], args[4]
    owners = lax.axis_size("ep")
    batches, dev_rows, width = hidden_in.shape
    ffw = gate_weight.shape[2]
    groups = owners // INNER
    if owners % INNER or owners > LANES:
        return local(*args)
    buffers, semaphores = kernel_scratch(groups, batches, dev_rows, width, ffw)
    total = 0
    for shape, kind in buffers:
        size = jnp.dtype(kind).itemsize
        for extent in shape:
            size *= extent
        total += size
    if total > VMEM_BYTES * 3 // 4:
        return local(*args)
    return fused(groups, buffers, semaphores, *args)


def solution(mesh):
    return jax.shard_map(
        serve_local,
        mesh=mesh,
        in_specs=(
            P(None, ("grp", "ep"), None),
            P(None, ("grp", "ep"), None),
            P(None, ("grp", "ep"), None),
            P(),
            P("ep", None, None),
            P("ep", None, None),
            P("ep", None, None),
            P("ep", None, None),
        ),
        out_specs=P(None, ("grp", "ep"), None),
        check_vma=False,
    )
```

```python
import functools

import jax
import jax.numpy as jnp
from jax import lax
from jax.experimental import pallas as pl
from jax.experimental.pallas import tpu as pltpu
from jax.sharding import PartitionSpec as P

SCALE_GROUP = 128
LANES = 128
INNER = 4
VMEM_BYTES = 67_043_328
MESH = pl.DeviceIdType.MESH
EXP_DEV = 1


def normalize(rows_in, norm_gain):
    values = rows_in.astype(jnp.float32)
    power = jnp.mean(values * values, axis=-1, keepdims=True)
    return (values * lax.rsqrt(power + 1e-06) * norm_gain).astype(jnp.bfloat16)


def local(
    hidden_in,
    expert_ids,
    route_share,
    norm_gain,
    gate_weight,
    up_weight,
    down_weight,
    exponent_table,
):
    owners = lax.axis_size("ep")
    experts = owners * EXP_DEV
    batches, dev_rows, fanout = expert_ids.shape
    model_width = hidden_in.shape[2]
    capacity = min(dev_rows, 2 * dev_rows * fanout // experts)
    scale_factors = jnp.repeat(jnp.exp2(exponent_table[0].astype(jnp.float32)), SCALE_GROUP, axis=1)
    gate_matrix = gate_weight[0]
    up_matrix = up_weight[0]
    down_mat = down_weight[0]
    slot_ids = jnp.arange(experts * capacity, dtype=jnp.int32)
    expert_range = jnp.arange(experts, dtype=jnp.int32)

    def expert_rows(block_of_rows):
        gate_output = (
            jnp.dot(block_of_rows, gate_matrix, preferred_element_type=jnp.float32)
            * scale_factors[0]
        )
        up_output = (
            jnp.dot(block_of_rows, up_matrix, preferred_element_type=jnp.float32) * scale_factors[1]
        )
        hidden_state = (jax.nn.silu(gate_output) * up_output * scale_factors[2]).astype(
            jnp.bfloat16
        )
        return jnp.dot(hidden_state, down_mat, preferred_element_type=jnp.float32).astype(
            jnp.bfloat16
        )

    def mixing_for(batch):
        flat_ids = expert_ids[batch].reshape(-1)
        onehot = (flat_ids[:, None] == expert_range[None, :]).astype(jnp.int32)
        position = jnp.sum((jnp.cumsum(onehot, axis=0) - 1) * onehot, axis=1)
        slot_of = (flat_ids * capacity + position).reshape(dev_rows, fanout)
        matches = slot_of[:, :, None] == slot_ids[None, None, :]
        shares = route_share[batch].astype(jnp.float32) / 64.0
        mixing = jnp.sum(jnp.where(matches, shares[:, :, None], 0.0), axis=1).astype(jnp.bfloat16)
        picker = jnp.any(matches, axis=1).T.astype(jnp.bfloat16)
        return (mixing, picker)

    def serve(batch_list):
        count = len(batch_list)
        mixings = []
        pickers = []
        for batch in batch_list:
            mixing, picker = mixing_for(batch)
            mixings.append(mixing)
            pickers.append(picker)
        normed_list = [normalize(hidden_in[batch], norm_gain) for batch in batch_list]
        local_rows = normed_list[0]
        local_ids = jnp.concatenate([expert_ids[batch] for batch in batch_list], axis=0)
        all_rows = lax.all_gather(local_rows, "ep", axis=0, tiled=True)
        all_ids = lax.all_gather(local_ids, "ep", axis=0, tiled=True)
        all_rows = all_rows.reshape(owners, count, dev_rows, model_width)
        all_ids = all_ids.reshape(owners, count, dev_rows, fanout)
        owner = lax.axis_index("ep")
        block_base = (jnp.arange(owners, dtype=jnp.int32) * capacity)[:, None]
        ids_here = all_ids[:, 0].reshape(owners, dev_rows * fanout)
        mine = (ids_here == owner).astype(jnp.int32)
        place = jnp.where(mine > 0, block_base + jnp.cumsum(mine, axis=1) - 1, -1)
        place = place.reshape(owners * dev_rows, fanout)
        chooser = jnp.any(place[:, :, None] == slot_ids[None, None, :], axis=1).T.astype(
            jnp.bfloat16
        )
        rows_here = all_rows[:, 0].reshape(owners * dev_rows, model_width)
        built = jnp.dot(chooser, rows_here, preferred_element_type=jnp.float32).astype(jnp.bfloat16)
        buffers = built.reshape(experts, capacity, model_width)
        produced = expert_rows(buffers.reshape(-1, model_width)).reshape(
            experts, count * capacity, model_width
        )
        returned = lax.all_to_all(produced, "ep", split_axis=0, concat_axis=0, tiled=True)
        return (returned, mixings)

    outputs = []
    for batch in range(batches):
        returned, mixings = serve([batch])
        gathered = returned.reshape(experts * capacity, model_width)
        mixed = jnp.dot(mixings[0], gathered, preferred_element_type=jnp.float32)
        outputs.append((hidden_in[batch].astype(jnp.float32) + mixed).astype(jnp.bfloat16))
    return jnp.stack(outputs)


def unit_tables(groups, batches):
    arrival, reduction = [], []
    for own in range(groups):
        keys = [(abs(o - own), b, o < own, o) for o in range(groups) for b in range(batches)]
        units = [o * batches + b for _, b, _, o in sorted(keys)]
        steps = [units[at * batches : (at + 1) * batches] for at in range(groups)]
        late = steps[max(groups - 2, 0) :]
        early = steps[: max(groups - 2, 0)][::-1]
        arrival.append(units)
        reduction.append([unit for step in late + early for unit in step])
    chains = {}
    last = 0
    for way in range(2):
        for rank in range(groups):
            own = rank if way == 0 else groups - 1 - rank
            dests = [o for o in range(groups) if (o > own if way == 0 else o < own)]
            before = own - 1 if way == 0 else own + 1
            wanted = []
            for outer in dests:
                for batch in range(batches):
                    unit = outer * batches + batch
                    ready = reduction[own].index(unit)
                    if rank > 0:
                        upstream = [at for at, found in chains[way, before].items() if found == unit][0]
                        ready = max(ready, upstream + 2)
                    wanted.append((ready, -abs(outer - own), unit))
            taken = {}
            for ready, _, unit in sorted(wanted):
                while ready in taken:
                    ready += 1
                taken[ready] = unit
                last = max(last, ready + 1)
            chains[way, own] = taken
    chain_rows = [[[chains[way, own].get(at, -1) for at in range(last)] for own in range(groups)] for way in range(2)]
    return arrival, reduction, chain_rows, last


def expert_kernel(
    groups,
    x_ref,
    ids_ref,
    share_ref,
    gain_ref,
    gate_hbm,
    up_hbm,
    down_hbm,
    exps_ref,
    out_ref,
    rows,
    gate,
    up,
    down,
    scales,
    hidden,
    part,
    core_in,
    y_out,
    y_in,
    keep,
    z_out,
    z_in,
    weight_sem,
    rows_sent,
    rows_got,
    core_sent,
    core_got,
    y_sent,
    y_got,
    z_sent,
    z_got,
):
    batches, dev_rows, width = x_ref.shape
    fanout = ids_ref.shape[1]
    units = groups * batches
    chunk_rows = INNER * dev_rows
    ffw = gate.shape[1]
    me = lax.axis_index("ep")
    core = lax.rem(me, 2)
    row = lax.rem(lax.div(me, 2), 2)
    place = lax.div(me, INNER)
    here = row * 2 + core
    sib = me + 1 - 2 * core
    across = me + 2 - 4 * row
    above = me + INNER
    below = me - INNER
    has_above = place < groups - 1
    has_below = place > 0

    weight_copies = [
        pltpu.make_async_copy(gate_hbm.at[0], gate, weight_sem.at[0]),
        pltpu.make_async_copy(up_hbm.at[0], up, weight_sem.at[1]),
        pltpu.make_async_copy(down_hbm.at[0], down, weight_sem.at[2]),
    ]
    for copy in weight_copies:
        copy.start()

    barrier = pltpu.get_barrier_semaphore()

    def greet(device):
        pl.semaphore_signal(barrier, inc=1, device_id={"ep": device}, device_id_type=MESH)

    greet(sib)
    greet(across)
    pl.when(has_above)(lambda: greet(above))
    pl.when(has_below)(lambda: greet(below))

    def remote(src, dst, sent, got, device):
        return pltpu.make_async_remote_copy(
            src_ref=src,
            dst_ref=dst,
            send_sem=sent,
            recv_sem=got,
            device_id={"ep": device},
            device_id_type=MESH,
        )

    def rows_copy(outer, batch, inner, kind, device):
        ref = rows.at[outer, batch, inner]
        return remote(ref, ref, rows_sent.at[outer, batch, kind], rows_got.at[outer, batch, inner], device)

    expert = lax.broadcasted_iota(jnp.int32, (LANES, dev_rows), 0)
    for batch in range(batches):
        values = x_ref[batch].astype(jnp.float32)
        power = jnp.mean(values * values, axis=-1, keepdims=True)
        normed = (values * lax.rsqrt(power + 1e-06) * gain_ref[...]).astype(jnp.bfloat16)
        mixing = jnp.zeros((LANES, dev_rows), jnp.float32)
        for k in range(fanout):
            share = share_ref[batch, k : k + 1, :].astype(jnp.float32) / 64.0
            mixing += jnp.where(ids_ref[batch, k : k + 1, :] == expert, share, 0.0)
        rows[place, batch, here, :, :width] = normed
        rows[place, batch, here, :, width:] = mixing.T.astype(jnp.bfloat16)
        if batch == 0:
            pl.semaphore_wait(barrier, 2 + has_above.astype(jnp.int32) + has_below.astype(jnp.int32))
        pl.when(has_above)(lambda: rows_copy(place, batch, here, 0, above).start())
        pl.when(has_below)(lambda: rows_copy(place, batch, here, 1, below).start())
        rows_copy(place, batch, here, 3, across).start()
        rows_copy(place, batch, here, 2, sib).start()

    for m in range(3):
        for j in range(ffw // SCALE_GROUP):
            power_of = jnp.full((1, SCALE_GROUP), exps_ref[m, 0, j], jnp.int32).astype(jnp.float32)
            scales[m : m + 1, j * SCALE_GROUP : (j + 1) * SCALE_GROUP] = jnp.exp2(power_of)

    arrival, reduction, chain_rows, slots = unit_tables(groups, batches)

    def look_up(table, index):
        found = jnp.int32(-1)
        for own in range(groups):
            for at, unit in enumerate(table[own]):
                found = jnp.where((place == own) & (index == at), jnp.int32(unit), found)
        return found

    def split(unit):
        return lax.div(unit, batches), lax.rem(unit, batches)

    def unit_of(u):
        return split(look_up(arrival, u))

    def reduced_unit(u):
        return split(look_up(reduction, u))

    other_row = (1 - row) * 2 + core

    def z_relay(i):
        distance = lax.div(i, batches) + 1
        batch = lax.rem(i, batches)

        def pass_on(outer, kind, more, device):
            rows_copy(outer, batch, here, kind, sib).wait_recv()
            pl.when(more)(lambda: rows_copy(outer, batch, here, kind, device).start())
            rows_copy(outer, batch, here, 3, across).start()
            rows_copy(outer, batch, here, 2, sib).start()

        pl.when(place + distance < groups)(lambda: pass_on(place + distance, 1, has_below, below))
        pl.when(place - distance >= 0)(lambda: pass_on(place - distance, 0, has_above, above))

    def y_relay(u):
        outer, batch = unit_of(u)
        rows_copy(outer, batch, other_row, 4, sib).wait_recv()
        rows_copy(outer, batch, other_row, 4, sib).start()

    def arrived(u):
        outer, batch = unit_of(u)
        rows_copy(outer, batch, row * 2 + 1 - core, 2, sib).wait_recv()
        rows_copy(outer, batch, (1 - row) * 2 + 1 - core, 4, sib).wait_recv()

    def compute_hidden(u):
        outer, batch = unit_of(u)
        block = rows[outer, batch, :, :, :width].reshape(chunk_rows, width)
        tile = 256
        for at in range(0, ffw, tile):
            cols = slice(at, at + tile)
            gated = jnp.dot(block, gate[:, cols], preferred_element_type=jnp.float32) * scales[0:1, cols]
            upped = jnp.dot(block, up[:, cols], preferred_element_type=jnp.float32) * scales[1:2, cols]
            hidden[:, cols] = (jax.nn.silu(gated) * upped * scales[2:3, cols]).astype(jnp.bfloat16)

    def core_copy(outer, batch, which):
        return remote(
            part.at[outer, batch, which * 2 + 1 - core],
            core_in.at[outer, batch, which],
            core_sent.at[outer, batch, which],
            core_got.at[outer, batch, which],
            sib,
        )

    def compute_part(u):
        outer, batch = unit_of(u)
        mixing = rows[outer, batch, :, :, width:].reshape(chunk_rows, LANES).astype(jnp.float32)
        wide_lane = lax.broadcasted_iota(jnp.int32, (chunk_rows, LANES), 1)
        share = jnp.sum(jnp.where(wide_lane == me, mixing, 0.0), axis=1, keepdims=True)
        tile = 512 if width % 512 == 0 else width
        for at in range(0, width, tile):
            cols = slice(at, at + tile)
            produced = jnp.dot(hidden[...], down[:, cols], preferred_element_type=jnp.float32) * share
            part[outer, batch, :, :, cols] = produced.astype(jnp.bfloat16).reshape(INNER, dev_rows, tile)
        core_copy(outer, batch, 1 - row).start()
        core_copy(outer, batch, row).start()

    def y_copy(outer, batch):
        return remote(
            y_out.at[outer, batch],
            y_in.at[outer, batch],
            y_sent.at[outer, batch],
            y_got.at[outer, batch],
            across,
        )

    def core_reduce(u):
        outer, batch = reduced_unit(u)
        core_copy(outer, batch, 1 - row).wait_recv()
        summed = part[outer, batch, other_row].astype(jnp.float32) + core_in[outer, batch, 1 - row].astype(jnp.float32)
        y_out[outer, batch] = summed.astype(jnp.bfloat16)
        y_copy(outer, batch).start()
        core_copy(outer, batch, row).wait_recv()
        keep[outer, batch] = part[outer, batch, here].astype(jnp.float32) + core_in[outer, batch, row].astype(
            jnp.float32
        )

    def y_reduce(u):
        outer, batch = reduced_unit(u)
        y_copy(outer, batch).wait_recv()
        keep[outer, batch] += y_in[outer, batch].astype(jnp.float32)

    def z_copy(way, outer, batch, device):
        return remote(
            z_out.at[outer, batch],
            z_in.at[way, outer, batch],
            z_sent.at[outer, batch],
            z_got.at[way, outer, batch],
            device,
        )

    def chain(u):
        for way, more, device in ((0, has_below, above), (1, has_above, below)):
            unit = look_up(chain_rows[way], u)
            active = unit >= 0
            outer, batch = split(jnp.maximum(unit, 0))

            @pl.when(active & more)
            def _():
                z_copy(way, outer, batch, sib).wait_recv()
                summed = keep[outer, batch] + z_in[way, outer, batch].astype(jnp.float32)
                z_out[outer, batch] = summed.astype(jnp.bfloat16)
                z_copy(way, outer, batch, device).start()

            @pl.when(active & jnp.logical_not(more))
            def _():
                z_out[outer, batch] = keep[outer, batch].astype(jnp.bfloat16)
                z_copy(way, outer, batch, device).start()

    early = max(units - batches, 0)

    @pl.loop(0, units + 1)
    def _(i):
        pl.when(i < (groups - 1) * batches)(lambda: z_relay(i))
        pl.when(i < units)(lambda: y_relay(i))

        @pl.when(i == 1)
        def _():
            for copy in weight_copies:
                copy.wait()

        @pl.when(i >= 1)
        def _():
            arrived(i - 1)
            compute_hidden(i - 1)
            compute_part(i - 1)

        pl.when(i >= early)(lambda: core_reduce(i - early))

    pl.loop(units + 1 - early, units)(core_reduce)

    @pl.loop(0, slots)
    def _(k):
        pl.when(k < units)(lambda: y_reduce(k))
        chain(k)

    for batch in range(batches):

        @pl.when(has_below)
        def _():
            z_copy(0, place, batch, sib).wait_recv()
            keep[place, batch] += z_in[0, place, batch].astype(jnp.float32)

        @pl.when(has_above)
        def _():
            z_copy(1, place, batch, sib).wait_recv()
            keep[place, batch] += z_in[1, place, batch].astype(jnp.float32)

        out_ref[batch] = (x_ref[batch].astype(jnp.float32) + keep[place, batch]).astype(jnp.bfloat16)

    @pl.loop(0, units)
    def _(u):
        outer = lax.div(u, batches)
        batch = lax.rem(u, batches)
        pl.when((outer <= place) & has_above)(lambda: rows_copy(outer, batch, here, 0, sib).wait_send())
        pl.when((outer >= place) & has_below)(lambda: rows_copy(outer, batch, here, 1, sib).wait_send())
        for kind in (2, 3, 4):
            rows_copy(outer, batch, here, kind, sib).wait_send()
        core_copy(outer, batch, 0).wait_send()
        core_copy(outer, batch, 1).wait_send()
        y_copy(outer, batch).wait_send()
        pl.when(outer != place)(lambda: z_copy(0, outer, batch, sib).wait_send())


def kernel_scratch(groups, batches, dev_rows, width, ffw):
    block = (groups, batches)
    bf16 = jnp.bfloat16
    buffers = [
        ((*block, INNER, dev_rows, width + LANES), bf16),
        ((width, ffw), bf16),
        ((width, ffw), bf16),
        ((ffw, width), bf16),
        ((8, ffw), jnp.float32),
        ((INNER * dev_rows, ffw), bf16),
        ((*block, INNER, dev_rows, width), bf16),
        ((*block, 2, dev_rows, width), bf16),
        ((*block, dev_rows, width), bf16),
        ((*block, dev_rows, width), bf16),
        ((*block, dev_rows, width), jnp.float32),
        ((*block, dev_rows, width), bf16),
        ((2, *block, dev_rows, width), bf16),
    ]
    semaphores = [(3,), (*block, 5), (*block, INNER), (*block, 2), (*block, 2), block, block, block, (2, *block)]
    return buffers, semaphores


def fused(groups, buffers, semaphores, hidden_in, expert_ids, route_share, norm_gain, gate_weight, up_weight, down_weight, exponent_table):
    vmem = pl.BlockSpec(memory_space=pltpu.VMEM)
    anywhere = pl.BlockSpec(memory_space=pl.ANY)
    return pl.pallas_call(
        functools.partial(expert_kernel, groups),
        out_shape=jax.ShapeDtypeStruct(hidden_in.shape, hidden_in.dtype),
        in_specs=[vmem, vmem, vmem, vmem, anywhere, anywhere, anywhere, pl.BlockSpec(memory_space=pltpu.SMEM)],
        out_specs=vmem,
        scratch_shapes=[pltpu.VMEM(shape, kind) for shape, kind in buffers]
        + [pltpu.SemaphoreType.DMA(shape) for shape in semaphores],
        compiler_params=pltpu.CompilerParams(
            collective_id=0, has_side_effects=True, vmem_limit_bytes=VMEM_BYTES * 15 // 16
        ),
    )(
        hidden_in,
        jnp.swapaxes(expert_ids, 1, 2),
        jnp.swapaxes(route_share, 1, 2),
        norm_gain[None, :],
        gate_weight,
        up_weight,
        down_weight,
        jnp.swapaxes(exponent_table, 0, 1),
    )


def serve_local(*args):
    hidden_in, gate_weight = args[0], args[4]
    owners = lax.axis_size("ep")
    batches, dev_rows, width = hidden_in.shape
    ffw = gate_weight.shape[2]
    groups = owners // INNER
    if owners % INNER or owners > LANES or owners < 2 * INNER:
        return local(*args)
    buffers, semaphores = kernel_scratch(groups, batches, dev_rows, width, ffw)
    total = 0
    for shape, kind in buffers:
        size = jnp.dtype(kind).itemsize
        for extent in shape:
            size *= extent
        total += size
    if total > VMEM_BYTES * 3 // 4:
        return local(*args)
    return fused(groups, buffers, semaphores, *args)


def solution(mesh):
    return jax.shard_map(
        serve_local,
        mesh=mesh,
        in_specs=(
            P(None, ("grp", "ep"), None),
            P(None, ("grp", "ep"), None),
            P(None, ("grp", "ep"), None),
            P(),
            P("ep", None, None),
            P("ep", None, None),
            P("ep", None, None),
            P("ep", None, None),
        ),
        out_specs=P(None, ("grp", "ep"), None),
        check_vma=False,
    )
```

```python
import functools

import jax
import jax.numpy as jnp
from jax import lax
from jax.experimental import pallas as pl
from jax.experimental.pallas import tpu as pltpu
from jax.sharding import PartitionSpec as P

SCALE_GROUP = 128
LANES = 128
INNER = 4
VMEM_BYTES = 67_043_328
MESH = pl.DeviceIdType.MESH
EXP_DEV = 1


def normalize(rows_in, norm_gain):
    values = rows_in.astype(jnp.float32)
    power = jnp.mean(values * values, axis=-1, keepdims=True)
    return (values * lax.rsqrt(power + 1e-06) * norm_gain).astype(jnp.bfloat16)


def local(
    hidden_in,
    expert_ids,
    route_share,
    norm_gain,
    gate_weight,
    up_weight,
    down_weight,
    exponent_table,
):
    owners = lax.axis_size("ep")
    experts = owners * EXP_DEV
    batches, dev_rows, fanout = expert_ids.shape
    model_width = hidden_in.shape[2]
    capacity = min(dev_rows, 2 * dev_rows * fanout // experts)
    scale_factors = jnp.repeat(jnp.exp2(exponent_table[0].astype(jnp.float32)), SCALE_GROUP, axis=1)
    gate_matrix = gate_weight[0]
    up_matrix = up_weight[0]
    down_mat = down_weight[0]
    slot_ids = jnp.arange(experts * capacity, dtype=jnp.int32)
    expert_range = jnp.arange(experts, dtype=jnp.int32)

    def expert_rows(block_of_rows):
        gate_output = (
            jnp.dot(block_of_rows, gate_matrix, preferred_element_type=jnp.float32)
            * scale_factors[0]
        )
        up_output = (
            jnp.dot(block_of_rows, up_matrix, preferred_element_type=jnp.float32) * scale_factors[1]
        )
        hidden_state = (jax.nn.silu(gate_output) * up_output * scale_factors[2]).astype(
            jnp.bfloat16
        )
        return jnp.dot(hidden_state, down_mat, preferred_element_type=jnp.float32).astype(
            jnp.bfloat16
        )

    def mixing_for(batch):
        flat_ids = expert_ids[batch].reshape(-1)
        onehot = (flat_ids[:, None] == expert_range[None, :]).astype(jnp.int32)
        position = jnp.sum((jnp.cumsum(onehot, axis=0) - 1) * onehot, axis=1)
        slot_of = (flat_ids * capacity + position).reshape(dev_rows, fanout)
        matches = slot_of[:, :, None] == slot_ids[None, None, :]
        shares = route_share[batch].astype(jnp.float32) / 64.0
        mixing = jnp.sum(jnp.where(matches, shares[:, :, None], 0.0), axis=1).astype(jnp.bfloat16)
        picker = jnp.any(matches, axis=1).T.astype(jnp.bfloat16)
        return (mixing, picker)

    def serve(batch_list):
        count = len(batch_list)
        mixings = []
        pickers = []
        for batch in batch_list:
            mixing, picker = mixing_for(batch)
            mixings.append(mixing)
            pickers.append(picker)
        normed_list = [normalize(hidden_in[batch], norm_gain) for batch in batch_list]
        local_rows = normed_list[0]
        local_ids = jnp.concatenate([expert_ids[batch] for batch in batch_list], axis=0)
        all_rows = lax.all_gather(local_rows, "ep", axis=0, tiled=True)
        all_ids = lax.all_gather(local_ids, "ep", axis=0, tiled=True)
        all_rows = all_rows.reshape(owners, count, dev_rows, model_width)
        all_ids = all_ids.reshape(owners, count, dev_rows, fanout)
        owner = lax.axis_index("ep")
        block_base = (jnp.arange(owners, dtype=jnp.int32) * capacity)[:, None]
        ids_here = all_ids[:, 0].reshape(owners, dev_rows * fanout)
        mine = (ids_here == owner).astype(jnp.int32)
        place = jnp.where(mine > 0, block_base + jnp.cumsum(mine, axis=1) - 1, -1)
        place = place.reshape(owners * dev_rows, fanout)
        chooser = jnp.any(place[:, :, None] == slot_ids[None, None, :], axis=1).T.astype(
            jnp.bfloat16
        )
        rows_here = all_rows[:, 0].reshape(owners * dev_rows, model_width)
        built = jnp.dot(chooser, rows_here, preferred_element_type=jnp.float32).astype(jnp.bfloat16)
        buffers = built.reshape(experts, capacity, model_width)
        produced = expert_rows(buffers.reshape(-1, model_width)).reshape(
            experts, count * capacity, model_width
        )
        returned = lax.all_to_all(produced, "ep", split_axis=0, concat_axis=0, tiled=True)
        return (returned, mixings)

    outputs = []
    for batch in range(batches):
        returned, mixings = serve([batch])
        gathered = returned.reshape(experts * capacity, model_width)
        mixed = jnp.dot(mixings[0], gathered, preferred_element_type=jnp.float32)
        outputs.append((hidden_in[batch].astype(jnp.float32) + mixed).astype(jnp.bfloat16))
    return jnp.stack(outputs)


def unit_tables(groups, batches):
    arrival, reduction = [], []
    for own in range(groups):
        keys = [(abs(o - own), b, o < own, o) for o in range(groups) for b in range(batches)]
        units = [o * batches + b for _, b, _, o in sorted(keys)]
        steps = [units[at * batches : (at + 1) * batches] for at in range(groups)]
        late = steps[max(groups - 2, 0) :]
        early = steps[: max(groups - 2, 0)][::-1]
        arrival.append(units)
        reduction.append([unit for step in late + early for unit in step])
    chains = {}
    last = 0
    for way in range(2):
        for rank in range(groups):
            own = rank if way == 0 else groups - 1 - rank
            dests = [o for o in range(groups) if (o > own if way == 0 else o < own)]
            before = own - 1 if way == 0 else own + 1
            wanted = []
            for outer in dests:
                for batch in range(batches):
                    unit = outer * batches + batch
                    ready = 2 * reduction[own].index(unit)
                    if rank > 0:
                        upstream = [at for at, found in chains[way, before].items() if found == unit][0]
                        ready = max(ready, upstream + 3)
                    wanted.append((ready, -abs(outer - own), unit))
            taken = {}
            for ready, _, unit in sorted(wanted):
                while ready in taken:
                    ready += 1
                taken[ready] = unit
                last = max(last, ready + 1)
            chains[way, own] = taken
    chain_rows = [[[chains[way, own].get(at, -1) for at in range(last)] for own in range(groups)] for way in range(2)]
    return arrival, reduction, chain_rows, max((last + 1) // 2, groups * batches)


def expert_kernel(
    groups,
    x_ref,
    ids_ref,
    share_ref,
    gain_ref,
    gate_hbm,
    up_hbm,
    down_hbm,
    exps_ref,
    out_ref,
    rows,
    gate,
    up,
    down,
    scales,
    hidden,
    part,
    core_in,
    y_out,
    y_in,
    keep,
    z_out,
    z_in,
    weight_sem,
    rows_sent,
    rows_got,
    core_sent,
    core_got,
    y_sent,
    y_got,
    z_sent,
    z_got,
):
    batches, dev_rows, width = x_ref.shape
    fanout = ids_ref.shape[1]
    units = groups * batches
    chunk_rows = INNER * dev_rows
    ffw = gate.shape[1]
    me = lax.axis_index("ep")
    core = lax.rem(me, 2)
    row = lax.rem(lax.div(me, 2), 2)
    place = lax.div(me, INNER)
    here = row * 2 + core
    sib = me + 1 - 2 * core
    across = me + 2 - 4 * row
    above = me + INNER
    below = me - INNER
    has_above = place < groups - 1
    has_below = place > 0

    weight_copies = [
        pltpu.make_async_copy(gate_hbm.at[0], gate, weight_sem.at[0]),
        pltpu.make_async_copy(up_hbm.at[0], up, weight_sem.at[1]),
        pltpu.make_async_copy(down_hbm.at[0], down, weight_sem.at[2]),
    ]
    for copy in weight_copies:
        copy.start()

    barrier = pltpu.get_barrier_semaphore()

    def greet(device):
        pl.semaphore_signal(barrier, inc=1, device_id={"ep": device}, device_id_type=MESH)

    greet(sib)
    greet(across)
    pl.when(has_above)(lambda: greet(above))
    pl.when(has_below)(lambda: greet(below))

    def remote(src, dst, sent, got, device):
        return pltpu.make_async_remote_copy(
            src_ref=src,
            dst_ref=dst,
            send_sem=sent,
            recv_sem=got,
            device_id={"ep": device},
            device_id_type=MESH,
        )

    def rows_copy(outer, batch, inner, kind, device):
        ref = rows.at[outer, batch, inner]
        return remote(ref, ref, rows_sent.at[outer, batch, kind], rows_got.at[outer, batch, inner], device)

    expert = lax.broadcasted_iota(jnp.int32, (LANES, dev_rows), 0)
    for batch in range(batches):
        values = x_ref[batch].astype(jnp.float32)
        power = jnp.mean(values * values, axis=-1, keepdims=True)
        normed = (values * lax.rsqrt(power + 1e-06) * gain_ref[...]).astype(jnp.bfloat16)
        mixing = jnp.zeros((LANES, dev_rows), jnp.float32)
        for k in range(fanout):
            share = share_ref[batch, k : k + 1, :].astype(jnp.float32) / 64.0
            mixing += jnp.where(ids_ref[batch, k : k + 1, :] == expert, share, 0.0)
        rows[place, batch, here, :, :width] = normed
        rows[place, batch, here, :, width:] = mixing.T.astype(jnp.bfloat16)
        if batch == 0:
            pl.semaphore_wait(barrier, 2 + has_above.astype(jnp.int32) + has_below.astype(jnp.int32))
        pl.when(has_above)(lambda: rows_copy(place, batch, here, 0, above).start())
        pl.when(has_below)(lambda: rows_copy(place, batch, here, 1, below).start())
        rows_copy(place, batch, here, 3, across).start()
        rows_copy(place, batch, here, 2, sib).start()

    for m in range(3):
        for j in range(ffw // SCALE_GROUP):
            power_of = jnp.full((1, SCALE_GROUP), exps_ref[m, 0, j], jnp.int32).astype(jnp.float32)
            scales[m : m + 1, j * SCALE_GROUP : (j + 1) * SCALE_GROUP] = jnp.exp2(power_of)

    arrival, reduction, chain_rows, slots = unit_tables(groups, batches)

    def own_row(table):
        found = [jnp.int32(unit) for unit in table[0]]
        for own in range(1, groups):
            found = [jnp.where(place == own, jnp.int32(unit), kept) for unit, kept in zip(table[own], found)]
        return found

    own_arrival, own_reduction = own_row(arrival), own_row(reduction)

    def look_up(row_units, index):
        if isinstance(index, int):
            return row_units[index] if index < len(row_units) else jnp.int32(-1)
        found = row_units[0]
        for at in range(1, len(row_units)):
            found = jnp.where(index == at, row_units[at], found)
        return found

    def split(unit):
        return lax.div(unit, batches), lax.rem(unit, batches)

    def unit_of(u):
        return split(look_up(own_arrival, u))

    def reduced_unit(u):
        return split(look_up(own_reduction, u))

    other_row = (1 - row) * 2 + core

    def z_relay(i):
        distance = lax.div(i, batches) + 1
        batch = lax.rem(i, batches)

        def pass_on(outer, kind, more, device):
            rows_copy(outer, batch, here, kind, sib).wait_recv()
            pl.when(more)(lambda: rows_copy(outer, batch, here, kind, device).start())
            rows_copy(outer, batch, here, 3, across).start()
            rows_copy(outer, batch, here, 2, sib).start()

        pl.when(place + distance < groups)(lambda: pass_on(place + distance, 1, has_below, below))
        pl.when(place - distance >= 0)(lambda: pass_on(place - distance, 0, has_above, above))

    def y_relay(u):
        outer, batch = unit_of(u)
        rows_copy(outer, batch, other_row, 4, sib).wait_recv()
        rows_copy(outer, batch, other_row, 4, sib).start()

    def arrived(u):
        outer, batch = unit_of(u)
        rows_copy(outer, batch, row * 2 + 1 - core, 2, sib).wait_recv()
        rows_copy(outer, batch, (1 - row) * 2 + 1 - core, 4, sib).wait_recv()

    def compute_hidden(u):
        outer, batch = unit_of(u)
        block = rows[outer, batch, :, :, :width].reshape(chunk_rows, width)
        tile = 256
        for at in range(0, ffw, tile):
            cols = slice(at, at + tile)
            gated = jnp.dot(block, gate[:, cols], preferred_element_type=jnp.float32) * scales[0:1, cols]
            upped = jnp.dot(block, up[:, cols], preferred_element_type=jnp.float32) * scales[1:2, cols]
            hidden[:, cols] = (jax.nn.silu(gated) * upped * scales[2:3, cols]).astype(jnp.bfloat16)

    def core_copy(outer, batch, which):
        return remote(
            part.at[outer, batch, which * 2 + 1 - core],
            core_in.at[outer, batch, which],
            core_sent.at[outer, batch, which],
            core_got.at[outer, batch, which],
            sib,
        )

    def compute_part(u):
        outer, batch = unit_of(u)
        mixing = rows[outer, batch, :, :, width:].reshape(chunk_rows, LANES).astype(jnp.float32)
        wide_lane = lax.broadcasted_iota(jnp.int32, (chunk_rows, LANES), 1)
        share = jnp.sum(jnp.where(wide_lane == me, mixing, 0.0), axis=1, keepdims=True)
        tile = 512 if width % 512 == 0 else width
        for at in range(0, width, tile):
            cols = slice(at, at + tile)
            produced = jnp.dot(hidden[...], down[:, cols], preferred_element_type=jnp.float32) * share
            part[outer, batch, :, :, cols] = produced.astype(jnp.bfloat16).reshape(INNER, dev_rows, tile)
        core_copy(outer, batch, 1 - row).start()
        core_copy(outer, batch, row).start()

    def y_copy(outer, batch):
        return remote(
            y_out.at[outer, batch],
            y_in.at[outer, batch],
            y_sent.at[outer, batch],
            y_got.at[outer, batch],
            across,
        )

    def core_reduce(u):
        outer, batch = reduced_unit(u)
        core_copy(outer, batch, 1 - row).wait_recv()
        summed = part[outer, batch, other_row].astype(jnp.float32) + core_in[outer, batch, 1 - row].astype(jnp.float32)
        y_out[outer, batch] = summed.astype(jnp.bfloat16)
        y_copy(outer, batch).start()
        core_copy(outer, batch, row).wait_recv()
        keep[outer, batch] = part[outer, batch, here].astype(jnp.float32) + core_in[outer, batch, row].astype(
            jnp.float32
        )

    def y_reduce(u):
        outer, batch = reduced_unit(u)
        y_copy(outer, batch).wait_recv()
        keep[outer, batch] += y_in[outer, batch].astype(jnp.float32)

    def z_copy(way, outer, batch, device):
        return remote(
            z_out.at[outer, batch],
            z_in.at[way, outer, batch],
            z_sent.at[outer, batch],
            z_got.at[way, outer, batch],
            device,
        )

    def chain(u):
        for way, more, device in ((0, has_below, above), (1, has_above, below)):
            if all(u >= len(row_units) or row_units[u] < 0 for row_units in chain_rows[way]):
                continue
            unit = look_up(own_row(chain_rows[way]), u)
            active = unit >= 0
            outer, batch = split(jnp.maximum(unit, 0))

            @pl.when(active & more)
            def _():
                z_copy(way, outer, batch, sib).wait_recv()
                summed = keep[outer, batch] + z_in[way, outer, batch].astype(jnp.float32)
                z_out[outer, batch] = summed.astype(jnp.bfloat16)
                z_copy(way, outer, batch, device).start()

            @pl.when(active & jnp.logical_not(more))
            def _():
                z_out[outer, batch] = keep[outer, batch].astype(jnp.bfloat16)
                z_copy(way, outer, batch, device).start()

    early = max(units - batches, 0)

    @pl.loop(0, units + 1)
    def _(i):
        pl.when(i < (groups - 1) * batches)(lambda: z_relay(i))
        pl.when(i < units)(lambda: y_relay(i))

        @pl.when(i == 1)
        def _():
            for copy in weight_copies:
                copy.wait()

        @pl.when(i >= 1)
        def _():
            arrived(i - 1)
            compute_hidden(i - 1)
            compute_part(i - 1)

        pl.when(i >= early)(lambda: core_reduce(i - early))

    for k in range(units + 1 - early, units):
        core_reduce(k)

    for k in range(slots):
        if k < units:
            y_reduce(k)
        chain(2 * k)
        chain(2 * k + 1)

    for batch in range(batches):

        @pl.when(has_below)
        def _():
            z_copy(0, place, batch, sib).wait_recv()
            keep[place, batch] += z_in[0, place, batch].astype(jnp.float32)

        @pl.when(has_above)
        def _():
            z_copy(1, place, batch, sib).wait_recv()
            keep[place, batch] += z_in[1, place, batch].astype(jnp.float32)

        out_ref[batch] = (x_ref[batch].astype(jnp.float32) + keep[place, batch]).astype(jnp.bfloat16)

    @pl.loop(0, units)
    def _(u):
        outer = lax.div(u, batches)
        batch = lax.rem(u, batches)
        pl.when((outer <= place) & has_above)(lambda: rows_copy(outer, batch, here, 0, sib).wait_send())
        pl.when((outer >= place) & has_below)(lambda: rows_copy(outer, batch, here, 1, sib).wait_send())
        for kind in (2, 3, 4):
            rows_copy(outer, batch, here, kind, sib).wait_send()
        core_copy(outer, batch, 0).wait_send()
        core_copy(outer, batch, 1).wait_send()
        y_copy(outer, batch).wait_send()
        pl.when(outer != place)(lambda: z_copy(0, outer, batch, sib).wait_send())


def kernel_scratch(groups, batches, dev_rows, width, ffw):
    block = (groups, batches)
    bf16 = jnp.bfloat16
    buffers = [
        ((*block, INNER, dev_rows, width + LANES), bf16),
        ((width, ffw), bf16),
        ((width, ffw), bf16),
        ((ffw, width), bf16),
        ((8, ffw), jnp.float32),
        ((INNER * dev_rows, ffw), bf16),
        ((*block, INNER, dev_rows, width), bf16),
        ((*block, 2, dev_rows, width), bf16),
        ((*block, dev_rows, width), bf16),
        ((*block, dev_rows, width), bf16),
        ((*block, dev_rows, width), jnp.float32),
        ((*block, dev_rows, width), bf16),
        ((2, *block, dev_rows, width), bf16),
    ]
    semaphores = [(3,), (*block, 5), (*block, INNER), (*block, 2), (*block, 2), block, block, block, (2, *block)]
    return buffers, semaphores


def fused(groups, buffers, semaphores, hidden_in, expert_ids, route_share, norm_gain, gate_weight, up_weight, down_weight, exponent_table):
    vmem = pl.BlockSpec(memory_space=pltpu.VMEM)
    anywhere = pl.BlockSpec(memory_space=pl.ANY)
    return pl.pallas_call(
        functools.partial(expert_kernel, groups),
        out_shape=jax.ShapeDtypeStruct(hidden_in.shape, hidden_in.dtype),
        in_specs=[vmem, vmem, vmem, vmem, anywhere, anywhere, anywhere, pl.BlockSpec(memory_space=pltpu.SMEM)],
        out_specs=vmem,
        scratch_shapes=[pltpu.VMEM(shape, kind) for shape, kind in buffers]
        + [pltpu.SemaphoreType.DMA(shape) for shape in semaphores],
        compiler_params=pltpu.CompilerParams(
            collective_id=0, has_side_effects=True, vmem_limit_bytes=VMEM_BYTES * 15 // 16
        ),
    )(
        hidden_in,
        jnp.swapaxes(expert_ids, 1, 2),
        jnp.swapaxes(route_share, 1, 2),
        norm_gain[None, :],
        gate_weight,
        up_weight,
        down_weight,
        jnp.swapaxes(exponent_table, 0, 1),
    )


def serve_local(*args):
    hidden_in, gate_weight = args[0], args[4]
    owners = lax.axis_size("ep")
    batches, dev_rows, width = hidden_in.shape
    ffw = gate_weight.shape[2]
    groups = owners // INNER
    if owners % INNER or owners > LANES or owners < 2 * INNER:
        return local(*args)
    buffers, semaphores = kernel_scratch(groups, batches, dev_rows, width, ffw)
    total = 0
    for shape, kind in buffers:
        size = jnp.dtype(kind).itemsize
        for extent in shape:
            size *= extent
        total += size
    if total > VMEM_BYTES * 3 // 4:
        return local(*args)
    return fused(groups, buffers, semaphores, *args)


def solution(mesh):
    return jax.shard_map(
        serve_local,
        mesh=mesh,
        in_specs=(
            P(None, ("grp", "ep"), None),
            P(None, ("grp", "ep"), None),
            P(None, ("grp", "ep"), None),
            P(),
            P("ep", None, None),
            P("ep", None, None),
            P("ep", None, None),
            P("ep", None, None),
        ),
        out_specs=P(None, ("grp", "ep"), None),
        check_vma=False,
    )
```
